256 devices in a mesh: grp: 32 (over z, x), nbr: 8 (over y, core).
Axes of the slice: x: 4, y: 4, z: 8, core: 2. Of those that a mesh axis runs over, the one named last changes fastest.
Arguments:
- gains: float32 [1024, 256, 256], P(('grp', 'nbr')), may hold values from -1 to 1
- covs: float32 [1024, 256, 256], P(('grp', 'nbr')), may hold values from -10 to 10, as said below
- terminal: float32 [256, 256], replicated, may hold values from -4 to 4, as said below
Outputs:
- smoothed: float32 [1024, 256, 256], P(('grp', 'nbr'))
The draws below stay inside these ranges and needn't reach their ends.
Inputs may be any that keep to these rules, and one draw needn't show every extreme that they name: `covs`: each matrix is symmetric positive definite. `terminal`: symmetric positive definite.
All inputs are finite; a program needn't handle non-finite values.
Results may differ from the reference program's by a relative error of at most 0.0003.
Values sent between devices are 32-bit elements; how exact they have to be, the bound alone decides.
No kernel may reach another device: no remote copies, remote signals or barrier semaphores. Data moves between devices by JAX's collectives and lax.ppermute only.
A program may use at most 64 MiB of HBM per device.

```python
import math
import jax
import jax.numpy as jnp
from jax import lax

STATE_SIZE = 256
TIME_STEPS = 1024


def draw_gains(key, part):
    random_keys = jax.random.split(jax.random.fold_in(key, 11), 5)
    raw = jax.random.normal(random_keys[0], (TIME_STEPS, STATE_SIZE, STATE_SIZE), jnp.float32) * (0.25 / math.sqrt(STATE_SIZE))
    skew = raw - jnp.swapaxes(raw, 1, 2)
    identity_matrix = jnp.eye(STATE_SIZE, dtype=jnp.float32)
    rotate = jnp.linalg.solve(identity_matrix[None] - skew, identity_matrix[None] + skew)
    share = 1.0 / 8.0
    fast = jax.random.uniform(random_keys[1], (STATE_SIZE,)) < share
    fast_rate = jax.random.uniform(random_keys[2], (STATE_SIZE,), minval=1.0 / 50.0, maxval=1.0 / 30.0)
    rate = jnp.where(fast, fast_rate, 0.5 / TIME_STEPS)
    jitter = jax.random.uniform(random_keys[3], (TIME_STEPS, STATE_SIZE), minval=0.6, maxval=1.4)
    scale_factor = jnp.exp(-rate[None, :] * jitter)
    device_places = jax.random.randint(random_keys[4], (4,), 0, TIME_STEPS)
    sample_group = jnp.any(jnp.arange(TIME_STEPS)[:, None] == device_places[None, :], axis=1)
    scale_factor = scale_factor * jnp.where(sample_group, 0.75, 1.0)[:, None]
    return (scale_factor[:, :, None] * rotate).astype(jnp.float32)


def draw_covs(key, part):
    random_keys = jax.random.split(jax.random.fold_in(key, 23), 2)
    process_noise = jax.random.normal(random_keys[0], (TIME_STEPS, STATE_SIZE, STATE_SIZE), jnp.float32)
    inner_product = jnp.einsum('kij,klj->kil', process_noise, process_noise) / STATE_SIZE
    extra_term = jax.random.uniform(random_keys[1], (TIME_STEPS, STATE_SIZE), minval=0.5, maxval=1.5)
    square_matrix = inner_product + extra_term[:, :, None] * jnp.eye(STATE_SIZE, dtype=jnp.float32)[None]
    return (0.01 * square_matrix).astype(jnp.float32)


def draw_terminal(key, part):
    random_keys = jax.random.split(jax.random.fold_in(key, 37), 2)
    process_noise = jax.random.normal(random_keys[0], (STATE_SIZE, STATE_SIZE), jnp.float32)
    extra_term = jax.random.uniform(random_keys[1], (STATE_SIZE,), minval=0.5, maxval=1.5)
    return (0.5 * jnp.dot(process_noise, process_noise.T) / STATE_SIZE + jnp.diag(extra_term)).astype(jnp.float32)


def setup_inputs(seed: int = 0) -> dict:
    key_of = jax.random.split(jax.random.key(seed), 4)
    gains = draw_gains(jax.random.fold_in(key_of[3], 71), 0)
    covs = draw_covs(jax.random.fold_in(key_of[3], 71), 0)
    terminal = draw_terminal(jax.random.fold_in(key_of[3], 71), 0)
    return dict(gains=gains, covs=covs, terminal=terminal)


def reference(gains, covs, terminal):

    def advance(state, pair):
        gain, cov = pair
        left = jnp.dot(gain.astype(jnp.float32), state.astype(jnp.float32), precision=lax.Precision.HIGHEST, preferred_element_type=jnp.float32)
        nxt = lax.dot_general(left.astype(jnp.float32), gain.astype(jnp.float32), (((1,), (1,)), ((), ())), precision=lax.Precision.HIGHEST, preferred_element_type=jnp.float32) + cov
        return (nxt, nxt)
    _, result = lax.scan(advance, terminal, (gains, covs), reverse=True)
    return result
```

```python
import jax
import jax.numpy as jnp
from jax import lax
from jax.experimental import pallas as pl
from jax.experimental.pallas import tpu as pltpu
from jax.sharding import PartitionSpec as P

AXES = ("grp", "nbr")
F32 = jnp.float32
BF16 = jnp.bfloat16


def split(a):
    high = a.astype(BF16)
    return high, (a - high.astype(F32)).astype(BF16)


def dot(a, b, transposed):
    dims = (((1,), (1 if transposed else 0,)), ((), ()))
    return lax.dot_general(a, b, dims, preferred_element_type=F32)


def product(a, b, transposed=False):
    (ah, al), (bh, bl) = a, b
    return dot(ah, bh, transposed) + (dot(ah, bl, transposed) + dot(al, bh, transposed))


def apply(gain, state):
    return product(split(product(gain, split(state))), gain, True)


def compose(first, second):
    gain = split(first[0])
    return product(gain, split(second[0])), apply(gain, second[1]) + first[1]


def pair_of(ref):
    return ref[0], ref[1]


def put(ref, pair):
    ref[0] = pair[0]
    ref[1] = pair[1]


def choose(flag, a, b):
    return jax.tree.map(lambda x, y: jnp.where(flag, x, y), a, b)


def other_pair(core, near, far):
    return choose(core == 0, (near, far), (far, near))


def local_kernel(gains, covs, total):
    pairs = [(gains[k], covs[k]) for k in range(gains.shape[0])]
    while len(pairs) > 1:
        pairs = [compose(*pairs[i : i + 2]) if i + 1 < len(pairs) else pairs[i] for i in range(0, len(pairs), 2)]
    put(total, pairs[0])


def merge(later, mine, other):
    return compose(choose(later, other, mine), choose(later, mine, other))


def outgoing(core, pair):
    return jnp.where(core == 0, pair[0], pair[1])


def first_kernel(flags, mine, other, total, send):
    new = merge(flags[1] != 0, pair_of(mine), pair_of(other))
    put(total, new)
    send[...] = outgoing(flags[0], new)


def total_kernel(flags, mine, near, far, total, send):
    other = other_pair(flags[0], near[...], far[...])
    new = merge(flags[1] != 0, pair_of(mine), other)
    put(total, new)
    send[...] = outgoing(flags[0], new)


def state_kernel(flags, mine, near, far, terminal, send):
    other = other_pair(flags[0], near[...], far[...])
    own = pair_of(mine)
    later = flags[1] != 0
    first, second = choose(later, other, own), choose(later, own, other)
    state = apply(split(second[0]), terminal[...]) + second[1]
    state = apply(split(first[0]), state) + first[1]
    half = send.shape[0]
    send[...] = jnp.where(flags[0] == 0, state[:half], state[half:])


def first_suffix_kernel(flags, other, suffix):
    later = flags[1] != 0
    size = suffix.shape[1]
    rows = lax.broadcasted_iota(jnp.int32, (size, size), 0)
    cols = lax.broadcasted_iota(jnp.int32, (size, size), 1)
    suffix[0] = jnp.where(later, (rows == cols).astype(F32), other[0])
    suffix[1] = jnp.where(later, jnp.zeros((size, size), F32), other[1])


def suffix_kernel(flags, before, near, far, suffix):
    old = pair_of(before)
    new = compose(old, other_pair(flags[0], near[...], far[...]))
    put(suffix, choose(flags[1] != 0, old, new))


def prepare_kernel(gains, covs, suffix, gain_out, cov_out):
    pair = pair_of(suffix)
    for k in range(gains.shape[0] - 1, -1, -1):
        pair = compose((gains[k], covs[k]), pair)
        gain_out[k] = pair[0]
        cov_out[k] = pair[1]


def final_kernel(flags, gains, covs, near, far, terminal, out):
    first = flags[0] == 0
    top, bottom = choose(first, (near[...], far[...]), (far[...], near[...]))
    state = jnp.where(flags[1] != 0, terminal[...], jnp.concatenate([top, bottom], axis=0))
    state = split(state)
    for k in range(gains.shape[0]):
        gain = split(gains[k])
        out[k] = product(split(product(gain, state)), gain, True) + covs[k]


def call(kernel, outs, products, flags, *args):
    vmem = pl.BlockSpec(memory_space=pltpu.VMEM)
    smem = [] if flags is None else [pl.BlockSpec(memory_space=pltpu.SMEM)]
    args = args if flags is None else (flags, *args)
    shapes = [jax.ShapeDtypeStruct(shape, F32) for shape in outs]
    width = outs[0][-1]
    return pl.pallas_call(
        kernel,
        out_shape=shapes,
        in_specs=smem + [vmem] * (len(args) - len(smem)),
        out_specs=[vmem] * len(shapes),
        cost_estimate=pl.CostEstimate(
            flops=products * 6 * width**3, transcendentals=0, bytes_accessed=4 * width * width * products
        ),
        compiler_params=pltpu.CompilerParams(vmem_limit_bytes=48 * 2**20),
    )(*args)


def per_device(gains, covs, terminal):
    count, width, _ = gains.shape
    groups, near_count = lax.axis_size("grp"), lax.axis_size("nbr")
    devices = groups * near_count
    place = lax.axis_index("grp") * near_count + lax.axis_index("nbr")
    core = place & 1
    levels = devices.bit_length() - 1
    matrix, pair = (width, width), (2, width, width)

    def flags(level):
        return jnp.stack([core, (place >> level) & 1]).astype(jnp.int32)

    def swap(x, distance):
        return lax.ppermute(x, AXES, [(i, i ^ distance) for i in range(devices)])

    (total,) = call(local_kernel, [pair], 9, None, gains, covs)
    other = swap(total, 1)
    total, send = call(first_kernel, [pair, matrix], 3, flags(0), total, other)
    (suffix,) = call(first_suffix_kernel, [pair], 1, flags(0), other)
    for level in range(1, levels - 1):
        near = swap(send, 1 << level)
        far = swap(near, 1)
        if level < levels - 2:
            total, send = call(total_kernel, [pair, matrix], 3, flags(level), total, near, far)
        else:
            (send,) = call(state_kernel, [(width // 2, width)], 4, flags(level), total, near, far, terminal)
        (suffix,) = call(suffix_kernel, [pair], 3, flags(level), suffix, near, far)
    half = devices // 2
    row = half // 4
    lower = []
    for i in range(half, devices):
        upper, rest = divmod(i - half, row)
        lower.append((i, (3 - upper) * row + rest))
    near = lax.ppermute(send, AXES, lower)
    far = swap(near, 1)
    ready, added = call(prepare_kernel, [(count, width, width)] * 2, 3 * count, None, gains, covs, suffix)
    (out,) = call(
        final_kernel, [(count, width, width)], 2 * count, flags(levels - 1), ready, added, near, far, terminal
    )
    return out


def solution(mesh):
    placed = (P(AXES, None, None), P(AXES, None, None), P())
    return jax.shard_map(
        per_device,
        mesh=mesh,
        in_specs=placed,
        out_specs=P(AXES, None, None),
        check_vma=False,
    )
```

```python
from functools import partial

import jax
import jax.numpy as jnp
from jax import lax
from jax.experimental import pallas as pl
from jax.experimental.pallas import tpu as pltpu
from jax.sharding import PartitionSpec as P

AXES = ("grp", "nbr")
F32 = jnp.float32
BF16 = jnp.bfloat16
TAIL = 8


def split(a):
    high = a.astype(BF16)
    return high, (a - high.astype(F32)).astype(BF16)


def dot(a, b, transposed):
    dims = (((1,), (1 if transposed else 0,)), ((), ()))
    return lax.dot_general(a, b, dims, preferred_element_type=F32)


def product(a, b, transposed=False):
    (ah, al), (bh, bl) = a, b
    return dot(ah, bh, transposed) + (dot(ah, bl, transposed) + dot(al, bh, transposed))


def apply(pair, state):
    gain = split(pair[0])
    return product(split(product(gain, split(state))), gain, True) + pair[1]


def compose(first, second):
    gain = split(first[0])
    mixed = split(product(gain, split(second[1])))
    return product(gain, split(second[0])), product(mixed, gain, True) + first[1]


def pair_of(ref):
    return ref[0], ref[1]


def put(ref, pair):
    ref[0] = pair[0]
    ref[1] = pair[1]


def choose(flag, a, b):
    return jax.tree.map(lambda x, y: jnp.where(flag, x, y), a, b)


def places(size):
    shape = (size, size)
    return lax.broadcasted_iota(jnp.int32, shape, 0), lax.broadcasted_iota(jnp.int32, shape, 1)


def identity_pair(size):
    rows, cols = places(size)
    return (rows == cols).astype(F32), jnp.zeros((size, size), F32)


def widen(block):
    half = block.shape[0] // 2
    return jnp.concatenate([block[:half], block[half:]], axis=1)


def narrow(rows):
    half = rows.shape[1] // 2
    return jnp.concatenate([rows[:, :half], rows[:, half:]], axis=0)


def pack(core, cov):
    half = cov.shape[0] // 2
    rows, cols = places(half)
    upper, across, lower = cov[:half, :half], cov[:half, half:], cov[half:, half:]
    both = jnp.where(rows >= cols, upper, lower)
    diagonal = jnp.sum(jnp.where(rows == cols, lower, 0.0), axis=0, keepdims=True)
    tail = jnp.broadcast_to(jnp.concatenate([diagonal, diagonal], axis=1), (TAIL, 2 * half))
    return jnp.concatenate([widen(jnp.where(core == 0, both, across)), tail], axis=0)


def unpack(first, second):
    rows_sent = first.shape[0] - TAIL
    both, across = narrow(first[:rows_sent]), narrow(second[:rows_sent])
    diagonal = first[rows_sent : rows_sent + 1, : both.shape[1]]
    rows, cols = places(both.shape[0])
    turned = both.T
    upper = jnp.where(rows >= cols, both, turned)
    lower = jnp.where(rows == cols, diagonal, jnp.where(rows < cols, both, turned))
    return jnp.concatenate(
        [jnp.concatenate([upper, across], axis=1), jnp.concatenate([across.T, lower], axis=1)], axis=0
    )


def message(core, pair):
    half = pair[0].shape[0] // 2
    return jnp.concatenate([jnp.where(core == 0, pair[0][:half], pair[0][half:]), pack(core, pair[1])], axis=0)


def received(core, near, far):
    first, second = choose(core == 0, (near[...], far[...]), (far[...], near[...]))
    half = first.shape[1] // 2
    return jnp.concatenate([first[:half], second[:half]], axis=0), unpack(first[half:], second[half:])


def local_kernel(flags, gains, covs, total, gain_buf, cov_buf, gain_sems, cov_sems):
    count = gain_buf.shape[0]
    copies = {}
    for k in range(0, count, 2):
        for name, at in (("g", k), ("c", k + 1), ("g", k + 1), ("c", k)):
            if at < count:
                source, buf, sems = (gains, gain_buf, gain_sems) if name == "g" else (covs, cov_buf, cov_sems)
                copies[name, at] = pltpu.make_async_copy(source.at[at], buf.at[at], sems.at[at])
                copies[name, at].start()
    pairs = []
    for k in range(0, count, 2):
        for at in range(k, min(k + 2, count)):
            copies["g", at].wait()
            copies["c", at].wait()
        now = [(gain_buf[at], cov_buf[at]) for at in range(k, min(k + 2, count))]
        pairs.append(compose(*now) if len(now) == 2 else now[0])
    while len(pairs) > 1:
        pairs = [compose(*pairs[i : i + 2]) if i + 1 < len(pairs) else pairs[i] for i in range(0, len(pairs), 2)]
    put(total, pairs[0])


def first_kernel(flags, mine, other, total, send):
    later = flags[0] != 0
    near, far = pair_of(mine), pair_of(other)
    new = compose(choose(later, far, near), choose(later, near, far))
    put(total, new)
    send[...] = message(flags[0], new)


def four_kernel(flags, mine, near, far, before, group, total, send, *, axis):
    place = flags[axis]
    rows = near.shape[0] // 3
    group[place] = mine[...]
    for d in range(1, 4):
        part = pl.ds((d - 1) * rows, rows)
        gain, cov = received(flags[0], near.at[part], far.at[part])
        group[place ^ d, 0] = gain
        group[place ^ d, 1] = cov
    first = compose(pair_of(group.at[0]), pair_of(group.at[1]))
    second = compose(pair_of(group.at[2]), pair_of(group.at[3]))
    put(group.at[2], second)
    new = compose(first, second)
    put(total, new)
    send[...] = message(flags[0], new)


def two_kernel(flags, mine, near, far, terminal, before, other, total, send, send_state, *, axis):
    late = received(flags[0], near, far)
    put(other, late)
    own = pair_of(mine)
    later = flags[axis] != 0
    first, second = choose(later, late, own), choose(later, own, late)
    new = compose(first, second)
    put(total, new)
    send[...] = message(flags[0], new)
    send_state[...] = pack(flags[0], apply(first, apply(second, terminal[...])))


def received_state(core, near, far):
    return unpack(*choose(core == 0, (near[...], far[...]), (far[...], near[...])))


def state_kernel(flags, mine, near, far, before, state, send):
    state[...] = received_state(flags[0], near, far)
    send[...] = pack(flags[0], apply(pair_of(mine), state[...]))


def first_suffix_kernel(flags, other, suffix):
    put(suffix, choose(flags[0] != 0, identity_pair(suffix.shape[1]), pair_of(other)))


def four_suffix_kernel(flags, before, group, suffix, *, axis):
    place = flags[axis]
    later = pair_of(group.at[2])
    whole = compose(pair_of(group.at[1]), later)
    step = choose(place == 0, whole, choose(place == 1, later, pair_of(group.at[3])))
    old = pair_of(before)
    put(suffix, choose(place == 3, old, compose(old, step)))


def two_suffix_kernel(flags, before, other, suffix, *, axis):
    old = pair_of(before)
    put(suffix, choose(flags[axis] != 0, old, compose(old, pair_of(other))))


def prepare_kernel(gains, covs, suffix, gain_out, cov_out):
    pair = pair_of(suffix)
    for k in range(gains.shape[0] - 1, -1, -1):
        pair = compose((gains[k], covs[k]), pair)
        gain_out[k] = pair[0]
        cov_out[k] = pair[1]


def final_kernel(flags, gains, covs, near, far, part_near, part_far, upper, terminal, out, buf, sems, *, axis):
    highest, high = flags[axis] != 0, flags[axis - 1] != 0
    low = received_state(flags[0], near, far)
    state = jnp.where(highest, jnp.where(high, terminal[...], upper[...]), low)
    moved = apply(received(flags[0], part_near, part_far), low)
    state = split(jnp.where(jnp.logical_or(highest, high), state, moved))
    copies = []
    for k in range(gains.shape[0]):
        gain = split(gains[k])
        buf[k] = product(split(product(gain, state)), gain, True) + covs[k]
        copies.append(pltpu.make_async_copy(buf.at[k], out.at[k], sems.at[k]))
        copies[-1].start()
    for copy in copies:
        copy.wait()


VMEM, SMEM, HBM = pltpu.VMEM, pltpu.SMEM, pltpu.HBM


def call(kernel, products, outs, args, scratch=()):
    width = outs[0][0][-1]
    placed = [x if space in (SMEM, pl.ANY) else pltpu.with_memory_space_constraint(x, space) for x, space in args]
    return pl.pallas_call(
        kernel,
        out_shape=[space(shape, F32) for shape, space in outs],
        in_specs=[pl.BlockSpec(memory_space=space) for _, space in args],
        out_specs=[pl.BlockSpec(memory_space=space) for _, space in outs],
        scratch_shapes=list(scratch),
        cost_estimate=pl.CostEstimate(
            flops=products * 6 * width**3, transcendentals=0, bytes_accessed=4 * width * width * products
        ),
        compiler_params=pltpu.CompilerParams(vmem_limit_bytes=12 * 2**20),
    )(*placed)


def per_device(gains, covs, terminal):
    count, width, _ = gains.shape
    groups, near_count = lax.axis_size("grp"), lax.axis_size("nbr")
    devices = groups * near_count
    place = lax.axis_index("grp") * near_count + lax.axis_index("nbr")
    bits = [(0, 1), (1, 3), (3, 3), (5, 1), (6, 1), (7, 1)]
    flags = jnp.stack([(place >> at) & mask for at, mask in bits]).astype(jnp.int32), SMEM
    pair, group = (2, width, width), (4, 2, width, width)
    packed = width // 4 + TAIL
    sent = (width // 2 + packed, width)
    stack = (count, width, width)

    def permute(x, pairs):
        return lax.ppermute(x, AXES, pairs)

    def swap(x):
        return permute(x, [(i, i ^ 1) for i in range(devices)])

    def inside(x):
        return x, VMEM

    sems = [pltpu.SemaphoreType.DMA((count,))]
    (total,) = call(
        local_kernel,
        9,
        [(pair, VMEM)],
        [flags, (gains, HBM), (covs, HBM)],
        [VMEM(stack, F32), VMEM(stack, F32)] + sems * 2,
    )
    other = swap(total)
    total, send = call(
        first_kernel, 3, [(pair, VMEM), (sent, VMEM)], [flags, inside(total), inside(other)]
    )
    (suffix,) = call(first_suffix_kernel, 1, [(pair, VMEM)], [flags, inside(other)])
    for axis in (1, 2):
        at = bits[axis][0]
        nears = [permute(send, [(i, i ^ (d << at)) for i in range(devices)]) for d in (1, 2, 3)]
        near = jnp.concatenate(nears, axis=0)
        near, suffix = lax.optimization_barrier((near, suffix))
        found, total, send = call(
            partial(four_kernel, axis=axis),
            9,
            [(group, VMEM), (pair, VMEM), (sent, VMEM)],
            [flags, inside(total), inside(near), inside(swap(near)), (suffix, pl.ANY)],
        )
        (suffix,) = call(
            partial(four_suffix_kernel, axis=axis), 6, [(pair, VMEM)], [flags, inside(suffix), inside(found)]
        )
    near = permute(send, [(i, i ^ 32) for i in range(devices)])
    near, suffix = lax.optimization_barrier((near, suffix))
    found, total, send, send_state = call(
        partial(two_kernel, axis=3),
        7,
        [(pair, VMEM), (pair, VMEM), (sent, VMEM), ((packed, width), VMEM)],
        [flags, inside(total), inside(near), inside(swap(near)), inside(terminal), (suffix, pl.ANY)],
    )
    (suffix,) = call(
        partial(two_suffix_kernel, axis=3), 3, [(pair, VMEM)], [flags, inside(suffix), inside(found)]
    )
    row = devices // 8
    near = permute(send_state, [(i, i - 2 * row) for i in range(6 * row, 8 * row)])
    near, suffix = lax.optimization_barrier((near, suffix))
    part_near = permute(send, [(i, i - 2 * row) for i in range(2 * row, 4 * row)])
    upper, send_state = call(
        state_kernel,
        2,
        [((width, width), VMEM), ((packed, width), VMEM)],
        [flags, inside(total), inside(near), inside(swap(near)), (suffix, pl.ANY)],
    )
    ready, added = call(
        prepare_kernel,
        3 * count,
        [(stack, VMEM), (stack, VMEM)],
        [inside(gains), inside(covs), inside(suffix)],
    )
    near = sum(
        permute(send_state, [((source * row) + i, (target * row) + i) for source, target in moves for i in range(row)])
        for moves in (((4, 3), (5, 2)), ((4, 1), (5, 0)))
    )
    near, part_near, ready, added = lax.optimization_barrier((near, part_near, ready, added))
    (out,) = call(
        partial(final_kernel, axis=5),
        2 * count,
        [(stack, HBM)],
        [
            flags,
            inside(ready),
            inside(added),
            inside(near),
            inside(swap(near)),
            inside(part_near),
            inside(swap(part_near)),
            inside(upper),
            inside(terminal),
        ],
        [VMEM(stack, F32)] + sems,
    )
    return out


def solution(mesh):
    placed = (P(AXES, None, None), P(AXES, None, None), P())
    return jax.shard_map(
        per_device,
        mesh=mesh,
        in_specs=placed,
        out_specs=P(AXES, None, None),
        check_vma=False,
    )
```

```python
from functools import partial

import jax
import jax.numpy as jnp
from jax import lax
from jax.experimental import pallas as pl
from jax.experimental.pallas import tpu as pltpu
from jax.sharding import PartitionSpec as P

AXES = ("grp", "nbr")
F32 = jnp.float32
BF16 = jnp.bfloat16
TAIL = 8


def split(a):
    high = a.astype(BF16)
    return high, (a - high.astype(F32)).astype(BF16)


def dot(a, b, transposed):
    dims = (((1,), (1 if transposed else 0,)), ((), ()))
    return lax.dot_general(a, b, dims, preferred_element_type=F32)


def product(a, b, transposed=False):
    (ah, al), (bh, bl) = a, b
    return dot(ah, bh, transposed) + (dot(ah, bl, transposed) + dot(al, bh, transposed))


def apply(pair, state):
    gain = split(pair[0])
    return product(split(product(gain, split(state))), gain, True) + pair[1]


def compose(first, second):
    gain = split(first[0])
    mixed = split(product(gain, split(second[1])))
    return product(gain, split(second[0])), product(mixed, gain, True) + first[1]


def pair_of(ref):
    return ref[0], ref[1]


def put(ref, pair):
    ref[0] = pair[0]
    ref[1] = pair[1]


def choose(flag, a, b):
    return jax.tree.map(lambda x, y: jnp.where(flag, x, y), a, b)


def places(size):
    shape = (size, size)
    return lax.broadcasted_iota(jnp.int32, shape, 0), lax.broadcasted_iota(jnp.int32, shape, 1)


def identity_pair(size):
    rows, cols = places(size)
    return (rows == cols).astype(F32), jnp.zeros((size, size), F32)


def widen(block):
    half = block.shape[0] // 2
    return jnp.concatenate([block[:half], block[half:]], axis=1)


def narrow(rows):
    half = rows.shape[1] // 2
    return jnp.concatenate([rows[:, :half], rows[:, half:]], axis=0)


def pack(core, cov):
    half = cov.shape[0] // 2
    rows, cols = places(half)
    upper, across, lower = cov[:half, :half], cov[:half, half:], cov[half:, half:]
    both = jnp.where(rows >= cols, upper, lower)
    diagonal = jnp.sum(jnp.where(rows == cols, lower, 0.0), axis=0, keepdims=True)
    tail = jnp.broadcast_to(jnp.concatenate([diagonal, diagonal], axis=1), (TAIL, 2 * half))
    return jnp.concatenate([widen(jnp.where(core == 0, both, across)), tail], axis=0)


def unpack(first, second):
    rows_sent = first.shape[0] - TAIL
    both, across = narrow(first[:rows_sent]), narrow(second[:rows_sent])
    diagonal = first[rows_sent : rows_sent + 1, : both.shape[1]]
    rows, cols = places(both.shape[0])
    turned = both.T
    upper = jnp.where(rows >= cols, both, turned)
    lower = jnp.where(rows == cols, diagonal, jnp.where(rows < cols, both, turned))
    return jnp.concatenate(
        [jnp.concatenate([upper, across], axis=1), jnp.concatenate([across.T, lower], axis=1)], axis=0
    )


def message(core, pair):
    half = pair[0].shape[0] // 2
    return jnp.concatenate([jnp.where(core == 0, pair[0][:half], pair[0][half:]), pack(core, pair[1])], axis=0)


def received(core, near, far):
    first, second = choose(core == 0, (near[...], far[...]), (far[...], near[...]))
    half = first.shape[1] // 2
    return jnp.concatenate([first[:half], second[:half]], axis=0), unpack(first[half:], second[half:])


def local_kernel(flags, gains, covs, total, gain_buf, cov_buf, gain_sems, cov_sems):
    count = gain_buf.shape[0]
    copies = {}
    for k in range(0, count, 2):
        for name, at in (("g", k), ("c", k + 1), ("g", k + 1), ("c", k)):
            if at < count:
                source, buf, sems = (gains, gain_buf, gain_sems) if name == "g" else (covs, cov_buf, cov_sems)
                copies[name, at] = pltpu.make_async_copy(source.at[at], buf.at[at], sems.at[at])
                copies[name, at].start()
    pairs = []
    for k in range(0, count, 2):
        for at in range(k, min(k + 2, count)):
            copies["g", at].wait()
            copies["c", at].wait()
        now = [(gain_buf[at], cov_buf[at]) for at in range(k, min(k + 2, count))]
        pairs.append(compose(*now) if len(now) == 2 else now[0])
    while len(pairs) > 1:
        pairs = [compose(*pairs[i : i + 2]) if i + 1 < len(pairs) else pairs[i] for i in range(0, len(pairs), 2)]
    put(total, pairs[0])


def first_kernel(flags, mine, other, total, send):
    later = flags[0] != 0
    near, far = pair_of(mine), pair_of(other)
    new = compose(choose(later, far, near), choose(later, near, far))
    put(total, new)
    send[...] = message(flags[0], new)


def four_kernel(flags, mine, near, far, before, group, total, send, *, axis):
    place = flags[axis]
    rows = near.shape[0] // 3
    group[place] = mine[...]
    for d in range(1, 4):
        part = pl.ds((d - 1) * rows, rows)
        gain, cov = received(flags[0], near.at[part], far.at[part])
        group[place ^ d, 0] = gain
        group[place ^ d, 1] = cov
    first = compose(pair_of(group.at[0]), pair_of(group.at[1]))
    second = compose(pair_of(group.at[2]), pair_of(group.at[3]))
    put(group.at[2], second)
    new = compose(first, second)
    put(total, new)
    send[...] = message(flags[0], new)


def two_kernel(flags, mine, near, far, terminal, before, other, total, send, send_state, *, axis):
    late = received(flags[0], near, far)
    put(other, late)
    own = pair_of(mine)
    later = flags[axis] != 0
    first, second = choose(later, late, own), choose(later, own, late)
    new = compose(first, second)
    put(total, new)
    send[...] = message(flags[0], new)
    send_state[...] = pack(flags[0], apply(first, apply(second, terminal[...])))


def received_state(core, near, far):
    return unpack(*choose(core == 0, (near[...], far[...]), (far[...], near[...])))


def state_kernel(flags, mine, near, far, before, state, send):
    state[...] = received_state(flags[0], near, far)
    send[...] = pack(flags[0], apply(pair_of(mine), state[...]))


def first_suffix_kernel(flags, other, suffix):
    put(suffix, choose(flags[0] != 0, identity_pair(suffix.shape[1]), pair_of(other)))


def four_suffix_kernel(flags, before, group, suffix, *, axis):
    place = flags[axis]
    later = pair_of(group.at[2])
    whole = compose(pair_of(group.at[1]), later)
    step = choose(place == 0, whole, choose(place == 1, later, pair_of(group.at[3])))
    old = pair_of(before)
    put(suffix, choose(place == 3, old, compose(old, step)))


def two_suffix_kernel(flags, before, other, suffix, *, axis):
    old = pair_of(before)
    put(suffix, choose(flags[axis] != 0, old, compose(old, pair_of(other))))


def prepare_kernel(gains, covs, suffix, gain_out, cov_out):
    pair = pair_of(suffix)
    for k in range(gains.shape[0] - 1, -1, -1):
        pair = compose((gains[k], covs[k]), pair)
        gain_out[k] = pair[0]
        cov_out[k] = pair[1]


def final_kernel(flags, gains, covs, near, far, upper, terminal, out, buf, sems, *, axis):
    highest, high = flags[axis] != 0, flags[axis - 1] != 0
    packed = gains.shape[1] // 4 + TAIL
    rows = near.shape[0] - packed
    part, rest = pl.ds(0, rows), pl.ds(rows, packed)
    low = received_state(flags[0], near.at[rest], far.at[rest])
    state = jnp.where(highest, jnp.where(high, terminal[...], upper[...]), low)
    moved = apply(received(flags[0], near.at[part], far.at[part]), low)
    state = split(jnp.where(jnp.logical_or(highest, high), state, moved))
    copies = []
    for k in range(gains.shape[0]):
        gain = split(gains[k])
        buf[k] = product(split(product(gain, state)), gain, True) + covs[k]
        copies.append(pltpu.make_async_copy(buf.at[k], out.at[k], sems.at[k]))
        copies[-1].start()
    for copy in copies:
        copy.wait()


VMEM, SMEM, HBM = pltpu.VMEM, pltpu.SMEM, pltpu.HBM


def call(kernel, products, outs, args, scratch=()):
    width = outs[0][0][-1]
    placed = [x if space in (SMEM, pl.ANY) else pltpu.with_memory_space_constraint(x, space) for x, space in args]
    return pl.pallas_call(
        kernel,
        out_shape=[space(shape, F32) for shape, space in outs],
        in_specs=[pl.BlockSpec(memory_space=space) for _, space in args],
        out_specs=[pl.BlockSpec(memory_space=space) for _, space in outs],
        scratch_shapes=list(scratch),
        cost_estimate=pl.CostEstimate(
            flops=products * 6 * width**3, transcendentals=0, bytes_accessed=4 * width * width * products
        ),
        compiler_params=pltpu.CompilerParams(vmem_limit_bytes=12 * 2**20),
    )(*placed)


def per_device(gains, covs, terminal):
    count, width, _ = gains.shape
    groups, near_count = lax.axis_size("grp"), lax.axis_size("nbr")
    devices = groups * near_count
    place = lax.axis_index("grp") * near_count + lax.axis_index("nbr")
    bits = [(0, 1), (1, 3), (3, 3), (5, 1), (6, 1), (7, 1)]
    flags = jnp.stack([(place >> at) & mask for at, mask in bits]).astype(jnp.int32), SMEM
    pair, group = (2, width, width), (4, 2, width, width)
    packed = width // 4 + TAIL
    sent = (width // 2 + packed, width)
    stack = (count, width, width)

    def permute(x, pairs):
        return lax.ppermute(x, AXES, pairs)

    def swap(x):
        return permute(x, [(i, i ^ 1) for i in range(devices)])

    def inside(x):
        return x, VMEM

    sems = [pltpu.SemaphoreType.DMA((count,))]
    (total,) = call(
        local_kernel,
        9,
        [(pair, VMEM)],
        [flags, (gains, HBM), (covs, HBM)],
        [VMEM(stack, F32), VMEM(stack, F32)] + sems * 2,
    )
    other = swap(total)
    total, send = call(
        first_kernel, 3, [(pair, VMEM), (sent, VMEM)], [flags, inside(total), inside(other)]
    )
    (suffix,) = call(first_suffix_kernel, 1, [(pair, VMEM)], [flags, inside(other)])
    for axis in (1, 2):
        at = bits[axis][0]
        nears = [permute(send, [(i, i ^ (d << at)) for i in range(devices)]) for d in (1, 2, 3)]
        near = jnp.concatenate(nears, axis=0)
        near, suffix = lax.optimization_barrier((near, suffix))
        found, total, send = call(
            partial(four_kernel, axis=axis),
            9,
            [(group, VMEM), (pair, VMEM), (sent, VMEM)],
            [flags, inside(total), inside(near), inside(swap(near)), (suffix, pl.ANY)],
        )
        (suffix,) = call(
            partial(four_suffix_kernel, axis=axis), 6, [(pair, VMEM)], [flags, inside(suffix), inside(found)]
        )
    near = permute(send, [(i, i ^ 32) for i in range(devices)])
    near, suffix = lax.optimization_barrier((near, suffix))
    found, total, send, send_state = call(
        partial(two_kernel, axis=3),
        7,
        [(pair, VMEM), (pair, VMEM), (sent, VMEM), ((packed, width), VMEM)],
        [flags, inside(total), inside(near), inside(swap(near)), inside(terminal), (suffix, pl.ANY)],
    )
    (suffix,) = call(
        partial(two_suffix_kernel, axis=3), 3, [(pair, VMEM)], [flags, inside(suffix), inside(found)]
    )
    row = devices // 8
    near = permute(send_state, [(i, i - 2 * row) for i in range(6 * row, 8 * row)])
    near, suffix = lax.optimization_barrier((near, suffix))
    part_near = permute(send, [(i, i - 2 * row) for i in range(2 * row, 4 * row)])
    upper, send_state = call(
        state_kernel,
        2,
        [((width, width), VMEM), ((packed, width), VMEM)],
        [flags, inside(total), inside(near), inside(swap(near)), (suffix, pl.ANY)],
    )
    ready, added = call(
        prepare_kernel,
        3 * count,
        [(stack, VMEM), (stack, VMEM)],
        [inside(gains), inside(covs), inside(suffix)],
    )
    near = sum(
        permute(send_state, [((source * row) + i, (target * row) + i) for source, target in moves for i in range(row)])
        for moves in (((4, 3), (5, 2)), ((4, 0), (5, 1)))
    )
    near, ready, added = lax.optimization_barrier((jnp.concatenate([part_near, near], axis=0), ready, added))
    (out,) = call(
        partial(final_kernel, axis=5),
        2 * count,
        [(stack, HBM)],
        [
            flags,
            inside(ready),
            inside(added),
            inside(near),
            inside(swap(near)),
            inside(upper),
            inside(terminal),
        ],
        [VMEM(stack, F32)] + sems,
    )
    return out


def solution(mesh):
    placed = (P(AXES, None, None), P(AXES, None, None), P())
    return jax.shard_map(
        per_device,
        mesh=mesh,
        in_specs=placed,
        out_specs=P(AXES, None, None),
        check_vma=False,
    )
```
